32 devices in a mesh: ch: 8 (over y, x, core), grp: 4 (over z).
Axes of the slice: x: 2, y: 2, z: 4, core: 2. Of those that a mesh axis runs over, the one named last changes fastest.
Arguments:
- raw: float32 [512, 4096], P(('ch', 'grp')), may hold values from -128 to 128, as said below
- fir_taps: float32 [129], replicated, may hold values from -4 to 4
- chan_map: int32 [4096], replicated, may hold values from 0 to 4095, each once
- order: int32 [3], replicated, may hold values from 0 to 31, as said below
Outputs:
- correlations: float32 [3, 32, 257, 4096], P(None, None, None, ('ch', 'grp'))
The draws below stay inside these ranges and needn't reach their ends.
Inputs may be any that keep to these rules, and one draw needn't show every extreme that they name: `order`: 3 distinct device indices; the device with flat index i over ch and grp holds regrouped channels i * 128 to (i + 1) * 128 - 1. `raw`: each time sample and each channel has its own scale.
All inputs are finite; a program needn't handle non-finite values.
Results may differ from the reference program's by a relative error of at most 0.0028.
Values may be sent and summed in bfloat16 or wider, within the bound.
No kernel may reach another device: no remote copies, remote signals or barrier semaphores. Data moves between devices by JAX's collectives and lax.ppermute only.
A program may use at most 128 MiB of HBM per device.

```python
import math
import jax
import jax.numpy as jnp
from jax import lax

CH_DEV = 128
FIR_HALF = 64
HALF = 128
SB = 32
STEPS = 3
TAPS = 129
OWNERS = 32
SAMPLES = 512
CHANNELS = 4096


def draw_raw(key, part):
    key_base, key_chan, key_time = jax.random.split(key, 3)
    chan_scale = jnp.exp(jax.random.uniform(key_chan, (1, CHANNELS), jnp.float32, 0.0, math.log(10.0)))
    time_scale = jnp.exp(jax.random.uniform(key_time, (SAMPLES, 1), jnp.float32, 0.0, math.log(3.2)))
    base = jnp.clip(jax.random.normal(key_base, (SAMPLES, CHANNELS), jnp.float32), -4.0, 4.0)
    return (base * chan_scale * time_scale).astype(jnp.float32)


def draw_order(key, part):
    key_mid, key_perm = jax.random.split(key, 2)
    middle = jax.random.permutation(key_mid, OWNERS - 2)[:STEPS - 2].astype(jnp.int32) + 1
    ends = jnp.array([0, OWNERS - 1], dtype=jnp.int32)
    values = jnp.concatenate([ends, middle])
    shuffle = jax.random.permutation(key_perm, STEPS)
    return values[shuffle].astype(jnp.int32)


def normal_values(stream_key, extent, spread, reach, kind=jnp.bfloat16):
    entries = spread * jax.random.normal(stream_key, extent, jnp.float32)
    return jnp.clip(entries, min=-reach, max=reach).astype(kind)


def setup_inputs(seed: int = 0) -> dict:
    key_list = jax.random.split(jax.random.key(seed), 5)
    raw = draw_raw(jax.random.fold_in(key_list[4], 71), 0)
    fir_taps = normal_values(key_list[1], (TAPS,), 1.0, 4.0, jnp.float32)
    chan_map = jax.random.permutation(key_list[2], CHANNELS).astype(jnp.int32)
    order = draw_order(jax.random.fold_in(key_list[4], 71), 0)
    return dict(raw=raw, fir_taps=fir_taps, chan_map=chan_map, order=order)


def reference(raw, fir_taps, chan_map, order):
    regrouped = jnp.take(raw, chan_map, axis=1).T[:, None, :]
    kernel = fir_taps[None, None, :]
    filtered = lax.conv_general_dilated(regrouped, kernel, (1,), [(FIR_HALF, FIR_HALF)], precision=lax.Precision.HIGHEST)[:, 0, :]
    power = lax.optimization_barrier(jnp.mean(filtered * filtered, axis=1, keepdims=True))
    whitened = (filtered / jnp.sqrt(power + 1e-06)).astype(jnp.bfloat16)
    receivers = whitened.astype(jnp.float32)[:, None, :]
    outputs = []
    for step in range(STEPS):
        start = (order[step] * CH_DEV).astype(jnp.int32)
        source = lax.dynamic_slice_in_dim(whitened, start, SB, 0).astype(jnp.float32)[:, None, :]
        corr = lax.conv_general_dilated(receivers, source, (1,), [(HALF, HALF)], precision=lax.Precision.HIGHEST)
        outputs.append(jnp.transpose(corr, (1, 2, 0)) / math.sqrt(SAMPLES))
    return jnp.stack(outputs)
```

```python
import functools
import math

import jax
import jax.numpy as jnp
from jax import lax
from jax.experimental import pallas as pl
from jax.experimental.pallas import tpu as pltpu
from jax.sharding import PartitionSpec as P

FIR_HALF = 64
HALF = 128
SB = 32
STEPS = 3
LAGS = 257
LANES = 128
SUB = 16
AXES = ("ch", "grp")


def regroup_kernel(order_ref, raw_ref, map_ref, out_ref, src_map):
    rows = raw_ref.shape[0]
    owners = map_ref.shape[0]
    width = src_map.shape[0]

    lane = lax.broadcasted_iota(jnp.int32, (width, LANES), 1)
    picked = jnp.zeros((width, LANES), jnp.int32)
    for step in range(STEPS):
        row = jnp.broadcast_to(map_ref[pl.ds(order_ref[step], 1), :], (width, LANES))
        if step:
            row = pltpu.roll(row, step * SB, 1)
        picked = jnp.where(lane // SB == step, row, picked)
    src_map[...] = picked

    def columns(where):
        tile = where // LANES
        spot = where % LANES
        parts = []
        for top in range(0, rows, width):
            taken = jnp.zeros((width, LANES), raw_ref.dtype)
            for block in range(owners):
                piece = raw_ref[top : top + width, block * LANES : (block + 1) * LANES]
                moved = jnp.take_along_axis(piece, spot, axis=1, mode="promise_in_bounds")
                taken = jnp.where(tile == block, moved, taken)
            parts.append(taken)
        return parts

    sources = columns(src_map[...])

    @pl.loop(0, owners)
    def _(dest):
        where = jnp.broadcast_to(map_ref[pl.ds(dest, 1), :], (width, LANES))
        own = columns(where)
        for index, top in enumerate(range(0, rows, width)):
            out_ref[dest, top : top + width, :LANES] = own[index].astype(out_ref.dtype)
            out_ref[dest, top : top + width, LANES:] = sources[index].astype(out_ref.dtype)


def regroup(raw, chan_map, order):
    rows, channels = raw.shape
    owners = channels // LANES
    return pl.pallas_call(
        regroup_kernel,
        out_shape=jax.ShapeDtypeStruct((owners, rows, 2 * LANES), jnp.float32),
        in_specs=[
            pl.BlockSpec(memory_space=pltpu.SMEM),
            pl.BlockSpec(memory_space=pltpu.VMEM),
            pl.BlockSpec(memory_space=pltpu.VMEM),
        ],
        out_specs=pl.BlockSpec(memory_space=pltpu.VMEM),
        scratch_shapes=[pltpu.VMEM((8, LANES), jnp.int32)],
        name="regroup",
    )(order, raw, chan_map.reshape(owners, LANES))


def split(value):
    high = value.astype(jnp.bfloat16)
    return high, (value - high.astype(jnp.float32)).astype(jnp.bfloat16)


def correlate_kernel(taps_ref, mixed_ref, out_ref, xh, xl, white, pair, turned, early, late, stage, sems):
    samples = mixed_ref.shape[0]

    def dot(a, b):
        return jnp.dot(a, b, preferred_element_type=jnp.float32)

    taps = jnp.broadcast_to(taps_ref[0:1, :], (LANES, 2 * LANES))
    band_h, band_l = split(pltpu.roll(taps, 0, 1, stride=1, stride_axis=0))
    edge = jnp.zeros((FIR_HALF, 2 * LANES), jnp.bfloat16)
    for ref in (xh, xl):
        ref[:FIR_HALF] = edge
        ref[FIR_HALF + samples :] = edge
    high, low = split(mixed_ref[...])
    xh[FIR_HALF : FIR_HALF + samples] = high
    xl[FIR_HALF : FIR_HALF + samples] = low
    power = jnp.zeros((1, 2 * LANES), jnp.float32)
    for start in range(0, samples, LANES):
        rows = slice(start, start + 2 * LANES)
        piece = dot(band_h, xh[rows]) + (dot(band_h, xl[rows]) + dot(band_l, xh[rows]))
        white[start : start + LANES] = piece
        power = power + jnp.sum(piece * piece, axis=0, keepdims=True)
    scale = 1.0 / jnp.sqrt(power * (1.0 / samples) + 1e-06)

    pair[...] = jnp.zeros_like(pair)
    own = (white[:, :LANES] * scale[:, :LANES]).astype(jnp.bfloat16)
    pair[HALF : HALF + samples, :LANES] = own
    pair[HALF - SUB : HALF - SUB + samples, LANES:] = own
    turned[...] = (white[:, LANES:] * scale[:, LANES:]).T

    lane = lax.broadcasted_iota(jnp.int32, (SB, samples), 1)
    gain = 1.0 / math.sqrt(samples)
    copies = []
    for step in range(STEPS):
        source = turned[step * SB : (step + 1) * SB]
        for shift in range(SUB):
            rows = slice(shift * SB, (shift + 1) * SB)
            moved = pltpu.roll(source, shift, 1) if shift else source
            late[rows] = jnp.where(lane >= shift, moved, 0.0).astype(jnp.bfloat16)
            back = SUB - shift
            moved = pltpu.roll(source, samples - back, 1)
            early[rows] = jnp.where(lane < samples - back, moved, 0.0).astype(jnp.bfloat16)
        for block in range(0, LAGS - 1, 2 * SUB):
            if block < HALF:
                part = dot(early[...], pair[block + SUB : block + SUB + samples])
            else:
                part = dot(late[...], pair[block : block + samples])
            part = part * gain
            stage[step, block : block + SUB] = part[:, :LANES].reshape(SUB, SB, LANES)
            stage[step, block + SUB : block + 2 * SUB] = part[:, LANES:].reshape(SUB, SB, LANES)
            lags = pl.ds(block, 2 * SUB)
            copies.append(pltpu.make_async_copy(stage.at[step, lags], out_ref.at[step, lags], sems.at[len(copies)]))
            copies[-1].start()
        last = dot(late[:SB], pair[2 * HALF : 2 * HALF + samples, :LANES]) * gain
        stage[step, LAGS - 1] = last
        lags = pl.ds(LAGS - 1, 1)
        copies.append(pltpu.make_async_copy(stage.at[step, lags], out_ref.at[step, lags], sems.at[len(copies)]))
        copies[-1].start()
    for copy in copies:
        copy.wait()


def correlate(fir_taps, mixed):
    samples = mixed.shape[0]
    taps = jnp.pad(fir_taps, (0, 2 * LANES - fir_taps.shape[0])).reshape(1, 2 * LANES)
    pieces = STEPS * ((LAGS - 1) // (2 * SUB) + 1)
    return pl.pallas_call(
        correlate_kernel,
        out_shape=jax.ShapeDtypeStruct((STEPS, LAGS, SB, LANES), jnp.float32),
        in_specs=[pl.BlockSpec(memory_space=pltpu.VMEM)] * 2,
        out_specs=pl.BlockSpec(memory_space=pl.ANY),
        scratch_shapes=[
            pltpu.VMEM((samples + 2 * FIR_HALF, 2 * LANES), jnp.bfloat16),
            pltpu.VMEM((samples + 2 * FIR_HALF, 2 * LANES), jnp.bfloat16),
            pltpu.VMEM((samples, 2 * LANES), jnp.float32),
            pltpu.VMEM((samples + 2 * HALF, 2 * LANES), jnp.bfloat16),
            pltpu.VMEM((LANES, samples), jnp.float32),
            pltpu.VMEM((SUB * SB, samples), jnp.bfloat16),
            pltpu.VMEM((SUB * SB, samples), jnp.bfloat16),
            pltpu.VMEM((STEPS, LAGS, SB, LANES), jnp.float32),
            pltpu.SemaphoreType.DMA((pieces,)),
        ],
        compiler_params=pltpu.CompilerParams(vmem_limit_bytes=48 * 1024 * 1024),
        name="correlate",
    )(taps, mixed)


def local(raw, fir_taps, chan_map, order):
    parts = regroup(raw, chan_map, order)
    mixed = lax.all_to_all(parts, AXES, split_axis=0, concat_axis=0, tiled=True)
    owners, rows, width = mixed.shape
    result = correlate(fir_taps, mixed.reshape(owners * rows, width))
    return jnp.transpose(result, (0, 2, 1, 3))


def solution(mesh):
    in_specs = (P(AXES, None), P(), P(), P())
    out_specs = P(None, None, None, AXES)
    return jax.shard_map(local, mesh=mesh, in_specs=in_specs, out_specs=out_specs, check_vma=False)
```

```python
import functools
import math

import jax
import jax.numpy as jnp
from jax import lax
from jax.experimental import pallas as pl
from jax.experimental.pallas import tpu as pltpu
from jax.sharding import PartitionSpec as P

FIR_HALF = 64
HALF = 128
SB = 32
STEPS = 3
LAGS = 257
LANES = 128
SUB = 16
GROUP = 4
CODES = 32767
OCTAVES = 32
FLOOR = -25
AXES = ("ch", "grp")


def encode(value):
    size = jnp.maximum(jnp.abs(value), 2.0**FLOOR)
    code = jnp.log(size) * (CODES / (OCTAVES * math.log(2.0))) + (0.5 - FLOOR * CODES / OCTAVES)
    code = jnp.minimum(code.astype(jnp.int32), CODES)
    return jnp.where(value < 0, -code, code)


def decode(code):
    size = jnp.exp(jnp.abs(code).astype(jnp.float32) * (OCTAVES * math.log(2.0) / CODES) + FLOOR * math.log(2.0))
    size = jnp.where(code == 0, 0.0, size)
    return jnp.where(code < 0, -size, size)


def regroup_kernel(order_ref, raw_ref, map_ref, out_ref, packed, src_map):
    rows = raw_ref.shape[0] // 2
    owners = map_ref.shape[0]
    packed[...] = (encode(raw_ref[rows:, :]) << 16) | (encode(raw_ref[:rows, :]) & 0xFFFF)

    lane = lax.broadcasted_iota(jnp.int32, (rows, LANES), 1)
    picked = jnp.zeros((rows, LANES), jnp.int32)
    for step in range(STEPS):
        row = jnp.broadcast_to(map_ref[pl.ds(order_ref[step], 1), :], (rows, LANES))
        if step:
            row = pltpu.roll(row, step * SB, 1)
        picked = jnp.where(lane // SB == step, row, picked)
    src_map[...] = picked

    def columns(where):
        tile = where // LANES
        spot = where % LANES
        taken = jnp.zeros((rows, LANES), jnp.int32)
        for block in range(owners):
            piece = packed[:, block * LANES : (block + 1) * LANES]
            moved = jnp.take_along_axis(piece, spot, axis=1, mode="promise_in_bounds")
            taken = jnp.where(tile == block, moved, taken)
        return taken

    sources = columns(src_map[...])

    @pl.loop(0, owners, step=GROUP)
    def _(first):
        for dest in range(GROUP):
            where = jnp.broadcast_to(map_ref[pl.ds(first + dest, 1), :], (rows, LANES))
            out_ref[first + dest, :, :LANES] = columns(where)
            out_ref[first + dest, :, LANES:] = sources


def regroup(raw, chan_map, order):
    rows, channels = raw.shape
    owners = channels // LANES
    return pl.pallas_call(
        regroup_kernel,
        out_shape=jax.ShapeDtypeStruct((owners, rows // 2, 2 * LANES), jnp.int32),
        in_specs=[
            pl.BlockSpec(memory_space=pltpu.SMEM),
            pl.BlockSpec(memory_space=pltpu.VMEM),
            pl.BlockSpec(memory_space=pltpu.VMEM),
        ],
        out_specs=pl.BlockSpec(memory_space=pltpu.VMEM),
        scratch_shapes=[pltpu.VMEM((rows // 2, channels), jnp.int32), pltpu.VMEM((rows // 2, LANES), jnp.int32)],
        name="regroup",
    )(order, raw, chan_map.reshape(owners, LANES))


def split(value):
    high = value.astype(jnp.bfloat16)
    return high, (value - high.astype(jnp.float32)).astype(jnp.bfloat16)


def correlate_kernel(taps_ref, mixed_ref, out_ref, xh, xl, white, pair, turned, early, late, stage, sems):
    owners, half, width = mixed_ref.shape
    samples = owners * half * 2

    def dot(a, b):
        return jnp.dot(a, b, preferred_element_type=jnp.float32)

    taps = jnp.broadcast_to(taps_ref[0:1, :], (LANES, 2 * LANES))
    band_h, band_l = split(pltpu.roll(taps, 0, 1, stride=1, stride_axis=0))
    edge = jnp.zeros((FIR_HALF, 2 * LANES), jnp.bfloat16)
    for ref in (xh, xl):
        ref[:FIR_HALF] = edge
        ref[FIR_HALF + samples :] = edge
    words = mixed_ref[...]
    values = jnp.concatenate([decode((words << 16) >> 16), decode(words >> 16)], axis=1)
    high, low = split(values.reshape(samples, width))
    xh[FIR_HALF : FIR_HALF + samples] = high
    xl[FIR_HALF : FIR_HALF + samples] = low
    power = jnp.zeros((1, 2 * LANES), jnp.float32)
    for start in range(0, samples, LANES):
        rows = slice(start, start + 2 * LANES)
        piece = dot(band_h, xh[rows]) + (dot(band_h, xl[rows]) + dot(band_l, xh[rows]))
        white[start : start + LANES] = piece
        power = power + jnp.sum(piece * piece, axis=0, keepdims=True)
    scale = 1.0 / jnp.sqrt(power * (1.0 / samples) + 1e-06)

    pair[...] = jnp.zeros_like(pair)
    own = (white[:, :LANES] * scale[:, :LANES]).astype(jnp.bfloat16)
    pair[HALF : HALF + samples, :LANES] = own
    pair[HALF - SUB : HALF - SUB + samples, LANES:] = own
    turned[...] = (white[:, LANES:] * scale[:, LANES:]).T

    lane = lax.broadcasted_iota(jnp.int32, (SB, samples), 1)
    gain = 1.0 / math.sqrt(samples)
    copies = []
    for step in range(STEPS):
        source = turned[step * SB : (step + 1) * SB]
        for shift in range(SUB):
            rows = slice(shift * SB, (shift + 1) * SB)
            moved = pltpu.roll(source, shift, 1) if shift else source
            late[rows] = jnp.where(lane >= shift, moved, 0.0).astype(jnp.bfloat16)
            back = SUB - shift
            moved = pltpu.roll(source, samples - back, 1)
            early[rows] = jnp.where(lane < samples - back, moved, 0.0).astype(jnp.bfloat16)
        for block in range(0, LAGS - 1, 2 * SUB):
            if block < HALF:
                part = dot(early[...], pair[block + SUB : block + SUB + samples])
            else:
                part = dot(late[...], pair[block : block + samples])
            part = part * gain
            stage[step, block : block + SUB] = part[:, :LANES].reshape(SUB, SB, LANES)
            stage[step, block + SUB : block + 2 * SUB] = part[:, LANES:].reshape(SUB, SB, LANES)
            lags = pl.ds(block, 2 * SUB)
            copies.append(pltpu.make_async_copy(stage.at[step, lags], out_ref.at[step, lags], sems.at[len(copies)]))
            copies[-1].start()
        last = dot(late[:SB], pair[2 * HALF : 2 * HALF + samples, :LANES]) * gain
        stage[step, LAGS - 1] = last
        lags = pl.ds(LAGS - 1, 1)
        copies.append(pltpu.make_async_copy(stage.at[step, lags], out_ref.at[step, lags], sems.at[len(copies)]))
        copies[-1].start()
    for copy in copies:
        copy.wait()


def correlate(fir_taps, mixed):
    owners, half, width = mixed.shape
    samples = owners * half * 2
    taps = jnp.pad(fir_taps, (0, 2 * LANES - fir_taps.shape[0])).reshape(1, 2 * LANES)
    pieces = STEPS * ((LAGS - 1) // (2 * SUB) + 1)
    return pl.pallas_call(
        correlate_kernel,
        out_shape=jax.ShapeDtypeStruct((STEPS, LAGS, SB, LANES), jnp.float32),
        in_specs=[pl.BlockSpec(memory_space=pltpu.VMEM)] * 2,
        out_specs=pl.BlockSpec(memory_space=pl.ANY),
        scratch_shapes=[
            pltpu.VMEM((samples + 2 * FIR_HALF, 2 * LANES), jnp.bfloat16),
            pltpu.VMEM((samples + 2 * FIR_HALF, 2 * LANES), jnp.bfloat16),
            pltpu.VMEM((samples, 2 * LANES), jnp.float32),
            pltpu.VMEM((samples + 2 * HALF, 2 * LANES), jnp.bfloat16),
            pltpu.VMEM((LANES, samples), jnp.float32),
            pltpu.VMEM((SUB * SB, samples), jnp.bfloat16),
            pltpu.VMEM((SUB * SB, samples), jnp.bfloat16),
            pltpu.VMEM((STEPS, LAGS, SB, LANES), jnp.float32),
            pltpu.SemaphoreType.DMA((pieces,)),
        ],
        compiler_params=pltpu.CompilerParams(vmem_limit_bytes=48 * 1024 * 1024),
        name="correlate",
    )(taps, mixed)


def local(raw, fir_taps, chan_map, order):
    parts = regroup(raw, chan_map, order)
    mixed = lax.all_to_all(parts, AXES, split_axis=0, concat_axis=0, tiled=True)
    result = correlate(fir_taps, mixed)
    return jnp.transpose(result, (0, 2, 1, 3))


def solution(mesh):
    in_specs = (P(AXES, None), P(), P(), P())
    out_specs = P(None, None, None, AXES)
    return jax.shard_map(local, mesh=mesh, in_specs=in_specs, out_specs=out_specs, check_vma=False)
```

```python
import functools
import math

import jax
import jax.numpy as jnp
from jax import lax
from jax.experimental import pallas as pl
from jax.experimental.pallas import tpu as pltpu
from jax.sharding import PartitionSpec as P

FIR_HALF = 64
HALF = 128
SB = 32
STEPS = 3
LAGS = 257
LANES = 128
SUB = 16
GROUP = 32
CODES = 32767
PARTS = 4
SENDS = ((0, 32), (32, 64), (64, 96), (96, 128), (128, 160), (160, 192), (192, 224), (224, 257))
OCTAVES = 32
FLOOR = -25
AXES = ("ch", "grp")


def encode(value):
    size = jnp.maximum(jnp.abs(value), 2.0**FLOOR)
    code = jnp.log(size) * (CODES / (OCTAVES * math.log(2.0))) + (0.5 - FLOOR * CODES / OCTAVES)
    code = jnp.minimum(code.astype(jnp.int32), CODES)
    return jnp.where(value < 0, -code, code)


def decode(code):
    size = jnp.exp(jnp.abs(code).astype(jnp.float32) * (OCTAVES * math.log(2.0) / CODES) + FLOOR * math.log(2.0))
    size = jnp.where(code == 0, 0.0, size)
    return jnp.where(code < 0, -size, size)


def regroup_kernel(order_ref, raw_ref, map_ref, out_ref, packed, src_map):
    rows = raw_ref.shape[0] // 2
    owners = map_ref.shape[0]
    packed[...] = (encode(raw_ref[rows:, :]) << 16) | (encode(raw_ref[:rows, :]) & 0xFFFF)

    lane = lax.broadcasted_iota(jnp.int32, (rows, LANES), 1)
    picked = jnp.zeros((rows, LANES), jnp.int32)
    for step in range(STEPS):
        row = jnp.broadcast_to(map_ref[pl.ds(order_ref[step], 1), :], (rows, LANES))
        if step:
            row = pltpu.roll(row, step * SB, 1)
        picked = jnp.where(lane // SB == step, row, picked)
    src_map[...] = picked

    def columns(where):
        tile = where // LANES
        spot = where % LANES
        taken = jnp.zeros((rows, LANES), jnp.int32)
        for block in range(owners):
            piece = packed[:, block * LANES : (block + 1) * LANES]
            moved = jnp.take_along_axis(piece, spot, axis=1, mode="promise_in_bounds")
            taken = jnp.where(tile == block, moved, taken)
        return taken

    sources = columns(src_map[...])

    @pl.loop(0, owners, step=GROUP)
    def _(first):
        for dest in range(GROUP):
            where = jnp.broadcast_to(map_ref[pl.ds(first + dest, 1), :], (rows, LANES))
            out_ref[first + dest, :, :LANES] = columns(where)
            out_ref[first + dest, :, LANES:] = sources


def regroup(raw, chan_map, order):
    rows, channels = raw.shape
    owners = channels // LANES
    return pl.pallas_call(
        regroup_kernel,
        out_shape=jax.ShapeDtypeStruct((owners, rows // 2, 2 * LANES), jnp.int32),
        in_specs=[
            pl.BlockSpec(memory_space=pltpu.SMEM),
            pl.BlockSpec(memory_space=pltpu.VMEM),
            pl.BlockSpec(memory_space=pltpu.VMEM),
        ],
        out_specs=pl.BlockSpec(memory_space=pltpu.VMEM),
        scratch_shapes=[pltpu.VMEM((rows // 2, channels), jnp.int32), pltpu.VMEM((rows // 2, LANES), jnp.int32)],
        name="regroup",
    )(order, raw, chan_map.reshape(owners, LANES))


def split(value):
    high = value.astype(jnp.bfloat16)
    return high, (value - high.astype(jnp.float32)).astype(jnp.bfloat16)


def correlate_kernel(taps_ref, mixed_ref, out_ref, xh, xl, white, pair, turned, left, stage, sems):
    owners, half, width = mixed_ref.shape
    samples = owners * half * 2

    def dot(a, b):
        return jnp.dot(a, b, preferred_element_type=jnp.float32)

    taps = jnp.broadcast_to(taps_ref[0:1, :], (LANES, 2 * LANES))
    band_h, band_l = split(pltpu.roll(taps, 0, 1, stride=1, stride_axis=0))
    edge = jnp.zeros((FIR_HALF, 2 * LANES), jnp.bfloat16)
    for ref in (xh, xl):
        ref[:FIR_HALF] = edge
        ref[FIR_HALF + samples :] = edge
    words = mixed_ref[...]
    values = jnp.concatenate([decode((words << 16) >> 16), decode(words >> 16)], axis=1)
    high, low = split(values.reshape(samples, width))
    xh[FIR_HALF : FIR_HALF + samples] = high
    xl[FIR_HALF : FIR_HALF + samples] = low
    power = jnp.zeros((1, 2 * LANES), jnp.float32)
    for start in range(0, samples, LANES):
        rows = slice(start, start + 2 * LANES)
        piece = dot(band_h, xh[rows]) + (dot(band_h, xl[rows]) + dot(band_l, xh[rows]))
        white[start : start + LANES] = piece
        power = power + jnp.sum(piece * piece, axis=0, keepdims=True)
    scale = 1.0 / jnp.sqrt(power * (1.0 / samples) + 1e-06)

    pair[...] = jnp.zeros_like(pair)
    own = (white[:, :LANES] * scale[:, :LANES]).astype(jnp.bfloat16)
    pair[HALF : HALF + samples, :LANES] = own
    pair[HALF - SUB : HALF - SUB + samples, LANES:] = own
    turned[:, :samples] = (white[:, LANES:] * scale[:, LANES:]).T.astype(jnp.bfloat16)
    turned[:, samples:] = jnp.zeros((LANES, LANES), jnp.bfloat16)

    gain = 1.0 / math.sqrt(samples)

    def build(step, late, shift):
        source = turned[pl.ds(pl.multiple_of(step * SB, SB), SB), :]
        amount = shift if late else samples + LANES - SUB + shift
        moved = pltpu.roll(source, amount, 1) if amount else source
        left[late, shift * SB : (shift + 1) * SB] = moved[:, :samples]

    def copy(step, index):
        start, stop = SENDS[index]
        lags = pl.ds(start, stop - start)
        return pltpu.make_async_copy(stage.at[step, lags], out_ref.at[step, lags], sems.at[step, index])

    for shift in range(SUB):
        build(0, 0, shift)
    blocks = HALF // (2 * SUB)
    deep = SUB // PARTS

    @pl.loop(0, STEPS)
    def _(step):
        for late in range(2):
            for index in range(blocks):
                block = late * HALF + index * 2 * SUB
                first = block if late else block + SUB
                for part in range(PARTS):
                    rows = slice(part * deep * SB, (part + 1) * deep * SB)
                    both = dot(left[late, rows], pair[first : first + samples]) * gain
                    low = block + part * deep
                    stage[step, low : low + deep] = both[:, :LANES].reshape(deep, SB, LANES)
                    stage[step, low + SUB : low + SUB + deep] = both[:, LANES:].reshape(deep, SB, LANES)
                if block + 2 * SUB == LAGS - 1:
                    last = dot(left[late, :SB], pair[2 * HALF : 2 * HALF + samples, :LANES])
                    stage[step, LAGS - 1] = last * gain
                for shift in range(index * SUB // blocks, (index + 1) * SUB // blocks):
                    build(step + late, 1 - late, shift)
                for piece, (_, stop) in enumerate(SENDS):
                    if stop in (block + 2 * SUB, block + 2 * SUB + 1):
                        copy(step, piece).start()

    for step in range(STEPS):
        for piece in range(len(SENDS)):
            copy(step, piece).wait()


def correlate(fir_taps, mixed):
    owners, half, width = mixed.shape
    samples = owners * half * 2
    taps = jnp.pad(fir_taps, (0, 2 * LANES - fir_taps.shape[0])).reshape(1, 2 * LANES)
    return pl.pallas_call(
        correlate_kernel,
        out_shape=jax.ShapeDtypeStruct((STEPS, LAGS, SB, LANES), jnp.float32),
        in_specs=[pl.BlockSpec(memory_space=pltpu.VMEM)] * 2,
        out_specs=pl.BlockSpec(memory_space=pl.ANY),
        scratch_shapes=[
            pltpu.VMEM((samples + 2 * FIR_HALF, 2 * LANES), jnp.bfloat16),
            pltpu.VMEM((samples + 2 * FIR_HALF, 2 * LANES), jnp.bfloat16),
            pltpu.VMEM((samples, 2 * LANES), jnp.float32),
            pltpu.VMEM((samples + 2 * HALF, 2 * LANES), jnp.bfloat16),
            pltpu.VMEM((LANES, samples + LANES), jnp.bfloat16),
            pltpu.VMEM((2, SUB * SB, samples), jnp.bfloat16),
            pltpu.VMEM((STEPS, LAGS, SB, LANES), jnp.float32),
            pltpu.SemaphoreType.DMA((STEPS, len(SENDS))),
        ],
        compiler_params=pltpu.CompilerParams(vmem_limit_bytes=48 * 1024 * 1024),
        name="correlate",
    )(taps, mixed)


def local(raw, fir_taps, chan_map, order):
    parts = regroup(raw, chan_map, order)
    mixed = lax.all_to_all(parts, AXES, split_axis=0, concat_axis=0, tiled=True)
    result = correlate(fir_taps, mixed)
    return jnp.transpose(result, (0, 2, 1, 3))


def solution(mesh):
    in_specs = (P(AXES, None), P(), P(), P())
    out_specs = P(None, None, None, AXES)
    return jax.shard_map(local, mesh=mesh, in_specs=in_specs, out_specs=out_specs, check_vma=False)
```

```python
import functools
import math

import jax
import jax.numpy as jnp
from jax import lax
from jax.experimental import pallas as pl
from jax.experimental.pallas import tpu as pltpu
from jax.sharding import PartitionSpec as P

FIR_HALF = 64
HALF = 128
SB = 32
STEPS = 3
LAGS = 257
LANES = 128
SUB = 16
GROUP = 32
CODES = 32767
HALF_ROWS = 8
PARTS = 4
SENDS = ((0, 32), (32, 64), (64, 96), (96, 128), (128, 160), (160, 192), (192, 224), (224, 257))
OCTAVES = 32
FLOOR = -25
AXES = ("ch", "grp")


def encode(value):
    size = jnp.maximum(jnp.abs(value), 2.0**FLOOR)
    code = jnp.log(size) * (CODES / (OCTAVES * math.log(2.0))) + (0.5 - FLOOR * CODES / OCTAVES)
    code = jnp.minimum(code.astype(jnp.int32), CODES)
    return jnp.where(value < 0, -code, code)


def decode(code):
    size = jnp.exp(jnp.abs(code).astype(jnp.float32) * (OCTAVES * math.log(2.0) / CODES) + FLOOR * math.log(2.0))
    size = jnp.where(code == 0, 0.0, size)
    return jnp.where(code < 0, -size, size)


def regroup_kernel(order_ref, raw_ref, map_ref, out_ref, packed):
    rows = raw_ref.shape[0] // 2
    owners = map_ref.shape[0]
    pitch = out_ref.shape[0] // owners
    packed[...] = (encode(raw_ref[rows:, :]) << 16) | (encode(raw_ref[:rows, :]) & 0xFFFF)

    lane = lax.broadcasted_iota(jnp.int32, (rows, LANES), 1)
    line = lax.broadcasted_iota(jnp.int32, (rows, LANES), 0)
    picked = jnp.zeros((rows, LANES), jnp.int32)
    for step in range(STEPS):
        row = jnp.broadcast_to(map_ref[pl.ds(order_ref[step], 1), :], (rows, LANES))
        if step:
            row = pltpu.roll(row, step * SB, 1)
        picked = jnp.where(lane // SB == step, row, picked)

    def columns(where):
        tile = where // LANES
        spot = where % LANES
        taken = jnp.zeros((rows, LANES), jnp.int32)
        for block in range(owners):
            piece = packed[:, block * LANES : (block + 1) * LANES]
            moved = jnp.take_along_axis(piece, spot, axis=1, mode="promise_in_bounds")
            taken = jnp.where(tile == block, moved, taken)
        return taken

    sources = columns(picked)
    kept = pitch - rows
    for target in range(kept):
        row, step = divmod(target, STEPS)
        moved = pltpu.roll(sources, LANES - (step + 1) * SB, 1)
        moved = jnp.broadcast_to(moved[kept + row : kept + row + 1], (rows, LANES))
        sources = jnp.where((line == target) & (lane >= STEPS * SB), moved, sources)

    @pl.loop(0, owners, step=GROUP)
    def _(first):
        start = pl.multiple_of(first * pitch, 8)
        for dest in range(GROUP):
            where = jnp.broadcast_to(map_ref[pl.ds(first + dest, 1), :], (rows, LANES))
            out_ref[pl.ds(start + dest * pitch, rows), :] = sources
            out_ref[pl.ds(start + dest * pitch + kept, rows), :] = columns(where)


def regroup(raw, chan_map, order):
    rows, channels = raw.shape
    owners = channels // LANES
    pitch = rows // 2 * (LANES + STEPS * SB) // LANES
    return pl.pallas_call(
        regroup_kernel,
        out_shape=jax.ShapeDtypeStruct((owners * pitch, LANES), jnp.int32),
        in_specs=[
            pl.BlockSpec(memory_space=pltpu.SMEM),
            pl.BlockSpec(memory_space=pltpu.VMEM),
            pl.BlockSpec(memory_space=pltpu.VMEM),
        ],
        out_specs=pl.BlockSpec(memory_space=pltpu.VMEM),
        scratch_shapes=[pltpu.VMEM((rows // 2, channels), jnp.int32)],
        name="regroup",
    )(order, raw, chan_map.reshape(owners, LANES))


def unpack(mixed_ref, words, owners):
    pitch = mixed_ref.shape[0] // owners
    rows = words.shape[1] // owners
    kept = pitch - rows
    for owner in range(owners):
        start = owner * pitch
        words[0, owner * rows : (owner + 1) * rows] = mixed_ref[start + kept : start + pitch, :]
        words[1, owner * rows : (owner + 1) * rows] = mixed_ref[start : start + rows, :]
    lane = lax.broadcasted_iota(jnp.int32, (owners, LANES), 1)
    for row in range(kept, rows):
        whole = jnp.zeros((owners, LANES), jnp.int32)
        for step in range(STEPS):
            target = (row - kept) * STEPS + step
            part = mixed_ref[pl.ds(target, owners, stride=pitch), :]
            part = pltpu.roll(part, (step + 1) * SB, 1)
            whole = jnp.where(lane // SB == step, part, whole)
        words[1, pl.ds(row, owners, stride=rows), :] = whole


def split(value):
    high = value.astype(jnp.bfloat16)
    return high, (value - high.astype(jnp.float32)).astype(jnp.bfloat16)


def correlate_kernel(taps_ref, mixed_ref, out_ref, fetched, xh, xl, white, pair, turned, left, stage, sems):
    half = fetched.shape[1]
    owners = half // HALF_ROWS
    samples = 2 * half
    unpack(mixed_ref, fetched, owners)

    def dot(a, b):
        return jnp.dot(a, b, preferred_element_type=jnp.float32)

    taps = jnp.broadcast_to(taps_ref[0:1, :], (LANES, 2 * LANES))
    band_h, band_l = split(pltpu.roll(taps, 0, 1, stride=1, stride_axis=0))
    edge = jnp.zeros((FIR_HALF, 2 * LANES), jnp.bfloat16)
    for ref in (xh, xl):
        ref[:FIR_HALF] = edge
        ref[FIR_HALF + samples :] = edge
    words = jnp.concatenate([fetched[0], fetched[1]], axis=1).reshape(owners, HALF_ROWS, 2 * LANES)
    values = jnp.concatenate([decode((words << 16) >> 16), decode(words >> 16)], axis=1)
    high, low = split(values.reshape(samples, 2 * LANES))
    xh[FIR_HALF : FIR_HALF + samples] = high
    xl[FIR_HALF : FIR_HALF + samples] = low
    power = jnp.zeros((1, 2 * LANES), jnp.float32)
    for start in range(0, samples, LANES):
        rows = slice(start, start + 2 * LANES)
        piece = dot(band_h, xh[rows]) + (dot(band_h, xl[rows]) + dot(band_l, xh[rows]))
        white[start : start + LANES] = piece
        power = power + jnp.sum(piece * piece, axis=0, keepdims=True)
    scale = 1.0 / jnp.sqrt(power * (1.0 / samples) + 1e-06)

    pair[...] = jnp.zeros_like(pair)
    own = (white[:, :LANES] * scale[:, :LANES]).astype(jnp.bfloat16)
    pair[HALF : HALF + samples, :LANES] = own
    pair[HALF - SUB : HALF - SUB + samples, LANES:] = own
    turned[:, :samples] = (white[:, LANES:] * scale[:, LANES:]).T.astype(jnp.bfloat16)
    turned[:, samples:] = jnp.zeros((LANES, LANES), jnp.bfloat16)

    gain = 1.0 / math.sqrt(samples)

    def build(step, late, shift):
        source = turned[pl.ds(step * SB, SB), :]
        amount = shift if late else samples + LANES - SUB + shift
        moved = pltpu.roll(source, amount, 1) if amount else source
        left[late, shift * SB : (shift + 1) * SB] = moved[:, :samples]

    def copy(step, index):
        start, stop = SENDS[index]
        lags = pl.ds(start, stop - start)
        return pltpu.make_async_copy(stage.at[step, lags], out_ref.at[step, lags], sems.at[step, index])

    for shift in range(SUB):
        build(0, 0, shift)
    blocks = HALF // (2 * SUB)
    deep = SUB // PARTS

    for step in range(STEPS):
        for late in range(2):
            for index in range(blocks):
                block = late * HALF + index * 2 * SUB
                first = block if late else block + SUB
                for part in range(PARTS):
                    rows = slice(part * deep * SB, (part + 1) * deep * SB)
                    both = dot(left[late, rows], pair[first : first + samples]) * gain
                    low = block + part * deep
                    stage[step, low : low + deep] = both[:, :LANES].reshape(deep, SB, LANES)
                    stage[step, low + SUB : low + SUB + deep] = both[:, LANES:].reshape(deep, SB, LANES)
                if block + 2 * SUB == LAGS - 1:
                    last = dot(left[late, :SB], pair[2 * HALF : 2 * HALF + samples, :LANES])
                    stage[step, LAGS - 1] = last * gain
                for shift in range(index * SUB // blocks, (index + 1) * SUB // blocks):
                    build(step + late, 1 - late, shift)
                for piece, (_, stop) in enumerate(SENDS):
                    if stop in (block + 2 * SUB, block + 2 * SUB + 1):
                        copy(step, piece).start()

    for step in range(STEPS):
        for piece in range(len(SENDS)):
            copy(step, piece).wait()


def correlate(fir_taps, mixed, samples):
    taps = jnp.pad(fir_taps, (0, 2 * LANES - fir_taps.shape[0])).reshape(1, 2 * LANES)
    return pl.pallas_call(
        correlate_kernel,
        out_shape=jax.ShapeDtypeStruct((STEPS, LAGS, SB, LANES), jnp.float32),
        in_specs=[pl.BlockSpec(memory_space=pltpu.VMEM)] * 2,
        out_specs=pl.BlockSpec(memory_space=pl.ANY),
        scratch_shapes=[
            pltpu.VMEM((2, samples // 2, LANES), jnp.int32),
            pltpu.VMEM((samples + 2 * FIR_HALF, 2 * LANES), jnp.bfloat16),
            pltpu.VMEM((samples + 2 * FIR_HALF, 2 * LANES), jnp.bfloat16),
            pltpu.VMEM((samples, 2 * LANES), jnp.float32),
            pltpu.VMEM((samples + 2 * HALF, 2 * LANES), jnp.bfloat16),
            pltpu.VMEM((LANES, samples + LANES), jnp.bfloat16),
            pltpu.VMEM((2, SUB * SB, samples), jnp.bfloat16),
            pltpu.VMEM((STEPS, LAGS, SB, LANES), jnp.float32),
            pltpu.SemaphoreType.DMA((STEPS, len(SENDS))),
        ],
        compiler_params=pltpu.CompilerParams(vmem_limit_bytes=48 * 1024 * 1024),
        name="correlate",
    )(taps, mixed)


def local(raw, fir_taps, chan_map, order):
    parts = regroup(raw, chan_map, order)
    rows, channels = raw.shape
    owners = channels // LANES
    parts = parts.reshape(owners, -1, 1, LANES)
    mixed = lax.all_to_all(parts, AXES, split_axis=0, concat_axis=0, tiled=True)
    result = correlate(fir_taps, mixed.reshape(-1, LANES), owners * rows)
    return jnp.transpose(result, (0, 2, 1, 3))


def solution(mesh):
    in_specs = (P(AXES, None), P(), P(), P())
    out_specs = P(None, None, None, AXES)
    return jax.shard_map(local, mesh=mesh, in_specs=in_specs, out_specs=out_specs, check_vma=False)
```

```python
import functools
import math

import jax
import jax.numpy as jnp
from jax import lax
from jax.experimental import pallas as pl
from jax.experimental.pallas import tpu as pltpu
from jax.sharding import PartitionSpec as P

FIR_HALF = 64
HALF = 128
SB = 32
STEPS = 3
LAGS = 257
LANES = 128
SUB = 16
GROUP = 32
CODES = 32767
HALF_ROWS = 8
PARTS = 4
SENDS = ((0, 32), (32, 64), (64, 96), (96, 128), (128, 160), (160, 192), (192, 224), (224, 257))
OCTAVES = 32
FLOOR = -25
AXES = ("ch", "grp")


def encode(value):
    size = jnp.maximum(jnp.abs(value), 2.0**FLOOR)
    code = jnp.log(size) * (CODES / (OCTAVES * math.log(2.0))) + (0.5 - FLOOR * CODES / OCTAVES)
    code = jnp.minimum(code.astype(jnp.int32), CODES)
    return jnp.where(value < 0, -code, code)


def decode(code):
    size = jnp.exp(jnp.abs(code).astype(jnp.float32) * (OCTAVES * math.log(2.0) / CODES) + FLOOR * math.log(2.0))
    size = jnp.where(code == 0, 0.0, size)
    return jnp.where(code < 0, -size, size)


def regroup_kernel(order_ref, raw_ref, map_ref, out_ref, packed):
    rows = raw_ref.shape[0] // 2
    owners = map_ref.shape[0]
    pitch = out_ref.shape[0] // owners
    packed[...] = (encode(raw_ref[rows:, :]) << 16) | (encode(raw_ref[:rows, :]) & 0xFFFF)

    lane = lax.broadcasted_iota(jnp.int32, (rows, LANES), 1)
    line = lax.broadcasted_iota(jnp.int32, (rows, LANES), 0)
    picked = jnp.zeros((rows, LANES), jnp.int32)
    for step in range(STEPS):
        row = jnp.broadcast_to(map_ref[pl.ds(order_ref[step], 1), :], (rows, LANES))
        if step:
            row = pltpu.roll(row, step * SB, 1)
        picked = jnp.where(lane // SB == step, row, picked)

    def columns(where):
        tile = where // LANES
        spot = where % LANES
        taken = jnp.zeros((rows, LANES), jnp.int32)
        for block in range(owners):
            piece = packed[:, block * LANES : (block + 1) * LANES]
            moved = jnp.take_along_axis(piece, spot, axis=1, mode="promise_in_bounds")
            taken = jnp.where(tile == block, moved, taken)
        return taken

    sources = columns(picked)
    kept = pitch - rows
    for target in range(kept):
        row, step = divmod(target, STEPS)
        moved = pltpu.roll(sources, LANES - (step + 1) * SB, 1)
        moved = jnp.broadcast_to(moved[kept + row : kept + row + 1], (rows, LANES))
        sources = jnp.where((line == target) & (lane >= STEPS * SB), moved, sources)

    @pl.loop(0, owners, step=GROUP)
    def _(first):
        start = pl.multiple_of(first * pitch, 8)
        for dest in range(GROUP):
            where = jnp.broadcast_to(map_ref[pl.ds(first + dest, 1), :], (rows, LANES))
            out_ref[pl.ds(start + dest * pitch, rows), :] = sources
            out_ref[pl.ds(start + dest * pitch + kept, rows), :] = columns(where)


def regroup(raw, chan_map, order):
    rows, channels = raw.shape
    owners = channels // LANES
    pitch = rows // 2 * (LANES + STEPS * SB) // LANES
    return pl.pallas_call(
        regroup_kernel,
        out_shape=jax.ShapeDtypeStruct((owners * pitch, LANES), jnp.int32),
        in_specs=[
            pl.BlockSpec(memory_space=pltpu.SMEM),
            pl.BlockSpec(memory_space=pltpu.VMEM),
            pl.BlockSpec(memory_space=pltpu.VMEM),
        ],
        out_specs=pl.BlockSpec(memory_space=pltpu.VMEM),
        scratch_shapes=[pltpu.VMEM((rows // 2, channels), jnp.int32)],
        name="regroup",
    )(order, raw, chan_map.reshape(owners, LANES))


def unpack(mixed_ref, words, owners):
    pitch = mixed_ref.shape[0] // owners
    rows = words.shape[1] // owners
    kept = pitch - rows
    for owner in range(owners):
        start = owner * pitch
        words[0, owner * rows : (owner + 1) * rows] = mixed_ref[start + kept : start + pitch, :]
        words[1, owner * rows : (owner + 1) * rows] = mixed_ref[start : start + rows, :]
    lane = lax.broadcasted_iota(jnp.int32, (owners, LANES), 1)
    for row in range(kept, rows):
        whole = jnp.zeros((owners, LANES), jnp.int32)
        for step in range(STEPS):
            target = (row - kept) * STEPS + step
            part = mixed_ref[pl.ds(target, owners, stride=pitch), :]
            part = pltpu.roll(part, (step + 1) * SB, 1)
            whole = jnp.where(lane // SB == step, part, whole)
        words[1, pl.ds(row, owners, stride=rows), :] = whole


def split(value):
    high = value.astype(jnp.bfloat16)
    return high, (value - high.astype(jnp.float32)).astype(jnp.bfloat16)


def correlate_kernel(taps_ref, mixed_ref, out_ref, fetched, xh, xl, white, pair, turned, left, stage, sems):
    half = fetched.shape[1]
    owners = half // HALF_ROWS
    samples = 2 * half
    unpack(mixed_ref, fetched, owners)

    def dot(a, b):
        return jnp.dot(a, b, preferred_element_type=jnp.float32)

    taps = jnp.broadcast_to(taps_ref[0:1, :], (LANES, 2 * LANES))
    band_h, band_l = split(pltpu.roll(taps, 0, 1, stride=1, stride_axis=0))
    band = jnp.concatenate([band_h, band_l, band_h], axis=1)
    edge = jnp.zeros((FIR_HALF, 2 * LANES), jnp.bfloat16)
    for ref in (xh, xl):
        ref[:FIR_HALF] = edge
        ref[FIR_HALF + samples :] = edge
    words = jnp.concatenate([fetched[0], fetched[1]], axis=1).reshape(owners, HALF_ROWS, 2 * LANES)
    values = jnp.concatenate([decode((words << 16) >> 16), decode(words >> 16)], axis=1)
    high, low = split(values.reshape(samples, 2 * LANES))
    xh[FIR_HALF : FIR_HALF + samples] = high
    xl[FIR_HALF : FIR_HALF + samples] = low
    power = jnp.zeros((1, 2 * LANES), jnp.float32)
    for start in range(0, samples, LANES):
        rows = slice(start, start + 2 * LANES)
        piece = dot(band, jnp.concatenate([xl[rows], xh[rows], xh[rows]], axis=0))
        white[start : start + LANES] = piece
        power = power + jnp.sum(piece * piece, axis=0, keepdims=True)
    scale = 1.0 / jnp.sqrt(power * (1.0 / samples) + 1e-06)

    for top in range(0, HALF, SUB):
        gap = jnp.zeros((SUB, 2 * LANES), jnp.bfloat16)
        pair[top : top + SUB] = gap
        pair[samples + HALF - SUB + top : samples + HALF + top] = gap
    pair[samples + 2 * HALF - SUB :] = jnp.zeros((SUB, 2 * LANES), jnp.bfloat16)
    own = (white[:, :LANES] * scale[:, :LANES]).astype(jnp.bfloat16)
    pair[HALF : HALF + samples, :LANES] = own
    pair[HALF - SUB : HALF - SUB + samples, LANES:] = own
    turned[:, :samples] = (white[:, LANES:] * scale[:, LANES:]).astype(jnp.bfloat16).T
    turned[:, samples:] = jnp.zeros((LANES, LANES), jnp.bfloat16)

    gain = 1.0 / math.sqrt(samples)

    def build(step, late, shift):
        source = turned[pl.ds(step * SB, SB), :]
        amount = shift if late else samples + LANES - SUB + shift
        moved = pltpu.roll(source, amount, 1) if amount else source
        left[late, shift * SB : (shift + 1) * SB] = moved[:, :samples]

    def copy(step, index):
        start, stop = SENDS[index]
        rows = pl.ds((step * LAGS + start) * SB, (stop - start) * SB)
        return pltpu.make_async_copy(stage.at[rows, :], out_ref.at[rows, :], sems.at[step, index])

    blocks = HALF // (2 * SUB)
    deep = SUB // PARTS

    for step in range(STEPS):
        for late in range(2):
            for index in range(blocks):
                block = late * HALF + index * 2 * SUB
                first = block if late else block + SUB
                for part in range(PARTS):
                    if step == late == index == 0:
                        for shift in range(part * deep, (part + 1) * deep):
                            build(0, 0, shift)
                    rows = slice(part * deep * SB, (part + 1) * deep * SB)
                    both = dot(left[late, rows], pair[first : first + samples]) * gain
                    low = block + part * deep
                    top = (step * LAGS + low) * SB
                    stage[top : top + deep * SB] = both[:, :LANES]
                    stage[top + SUB * SB : top + (SUB + deep) * SB] = both[:, LANES:]
                if block + 2 * SUB == LAGS - 1:
                    last = dot(left[late, :SB], pair[2 * HALF : 2 * HALF + samples, :LANES])
                    top = (step * LAGS + LAGS - 1) * SB
                    stage[top : top + SB] = last * gain
                for shift in range(index * SUB // blocks, (index + 1) * SUB // blocks):
                    build(step + late, 1 - late, shift)
                for piece, (_, stop) in enumerate(SENDS):
                    if stop in (block + 2 * SUB, block + 2 * SUB + 1):
                        copy(step, piece).start()

    for step in range(STEPS):
        for piece in range(len(SENDS)):
            copy(step, piece).wait()


def correlate(fir_taps, mixed, samples):
    taps = jnp.pad(fir_taps, (0, 2 * LANES - fir_taps.shape[0])).reshape(1, 2 * LANES)
    return pl.pallas_call(
        correlate_kernel,
        out_shape=jax.ShapeDtypeStruct((STEPS * LAGS * SB, LANES), jnp.float32),
        in_specs=[pl.BlockSpec(memory_space=pltpu.VMEM)] * 2,
        out_specs=pl.BlockSpec(memory_space=pl.ANY),
        scratch_shapes=[
            pltpu.VMEM((2, samples // 2, LANES), jnp.int32),
            pltpu.VMEM((samples + 2 * FIR_HALF, 2 * LANES), jnp.bfloat16),
            pltpu.VMEM((samples + 2 * FIR_HALF, 2 * LANES), jnp.bfloat16),
            pltpu.VMEM((samples, 2 * LANES), jnp.float32),
            pltpu.VMEM((samples + 2 * HALF, 2 * LANES), jnp.bfloat16),
            pltpu.VMEM((LANES, samples + LANES), jnp.bfloat16),
            pltpu.VMEM((2, SUB * SB, samples), jnp.bfloat16),
            pltpu.VMEM((STEPS * LAGS * SB, LANES), jnp.float32),
            pltpu.SemaphoreType.DMA((STEPS, len(SENDS))),
        ],
        compiler_params=pltpu.CompilerParams(vmem_limit_bytes=48 * 1024 * 1024),
        name="correlate",
    )(taps, mixed)


def local(raw, fir_taps, chan_map, order):
    parts = regroup(raw, chan_map, order)
    rows, channels = raw.shape
    owners = channels // LANES
    parts = parts.reshape(owners, -1, 1, LANES)
    mixed = lax.all_to_all(parts, AXES, split_axis=0, concat_axis=0, tiled=True)
    result = correlate(fir_taps, mixed.reshape(-1, LANES), owners * rows)
    return jnp.transpose(result.reshape(STEPS, LAGS, SB, LANES), (0, 2, 1, 3))


def solution(mesh):
    in_specs = (P(AXES, None), P(), P(), P())
    out_specs = P(None, None, None, AXES)
    return jax.shard_map(local, mesh=mesh, in_specs=in_specs, out_specs=out_specs, check_vma=False)
```

```python
import functools
import math

import jax
import jax.numpy as jnp
from jax import lax
from jax.experimental import pallas as pl
from jax.experimental.pallas import tpu as pltpu
from jax.sharding import PartitionSpec as P

FIR_HALF = 64
HALF = 128
SB = 32
STEPS = 3
LAGS = 257
LANES = 128
SUB = 16
GROUP = 32
CODES = 32767
HALF_ROWS = 8
PARTS = 4
SENDS = ((0, 32), (32, 64), (64, 96), (96, 128), (128, 160), (160, 192), (192, 224), (224, 257))
OCTAVES = 32
FLOOR = -25
AXES = ("ch", "grp")


def encode(value):
    size = jnp.maximum(jnp.abs(value), 2.0**FLOOR)
    code = jnp.log(size) * (CODES / (OCTAVES * math.log(2.0))) + (0.5 - FLOOR * CODES / OCTAVES)
    code = jnp.minimum(code.astype(jnp.int32), CODES)
    return jnp.where(value < 0, -code, code)


def decode(code):
    size = jnp.exp(jnp.abs(code).astype(jnp.float32) * (OCTAVES * math.log(2.0) / CODES) + FLOOR * math.log(2.0))
    size = jnp.where(code == 0, 0.0, size)
    return jnp.where(code < 0, -size, size)


def regroup_kernel(order_ref, raw_ref, map_ref, out_ref, packed):
    rows = raw_ref.shape[0] // 2
    owners = map_ref.shape[0]
    pitch = out_ref.shape[0] // owners
    packed[...] = (encode(raw_ref[rows:, :]) << 16) | (encode(raw_ref[:rows, :]) & 0xFFFF)

    lane = lax.broadcasted_iota(jnp.int32, (rows, LANES), 1)
    line = lax.broadcasted_iota(jnp.int32, (rows, LANES), 0)
    picked = jnp.zeros((rows, LANES), jnp.int32)
    for step in range(STEPS):
        row = jnp.broadcast_to(map_ref[pl.ds(order_ref[step], 1), :], (rows, LANES))
        if step:
            row = pltpu.roll(row, step * SB, 1)
        picked = jnp.where(lane // SB == step, row, picked)

    def columns(where):
        tile = where // LANES
        spot = where % LANES
        taken = jnp.zeros((rows, LANES), jnp.int32)
        for block in range(owners):
            piece = packed[:, block * LANES : (block + 1) * LANES]
            moved = jnp.take_along_axis(piece, spot, axis=1, mode="promise_in_bounds")
            taken = jnp.where(tile == block, moved, taken)
        return taken

    sources = columns(picked)
    kept = pitch - rows
    for target in range(kept):
        row, step = divmod(target, STEPS)
        moved = pltpu.roll(sources, LANES - (step + 1) * SB, 1)
        moved = jnp.broadcast_to(moved[kept + row : kept + row + 1], (rows, LANES))
        sources = jnp.where((line == target) & (lane >= STEPS * SB), moved, sources)

    @pl.loop(0, owners, step=GROUP)
    def _(first):
        start = pl.multiple_of(first * pitch, 8)
        for dest in range(GROUP):
            where = jnp.broadcast_to(map_ref[pl.ds(first + dest, 1), :], (rows, LANES))
            out_ref[pl.ds(start + dest * pitch, rows), :] = sources
            out_ref[pl.ds(start + dest * pitch + kept, rows), :] = columns(where)


def regroup(raw, chan_map, order):
    rows, channels = raw.shape
    owners = channels // LANES
    pitch = rows // 2 * (LANES + STEPS * SB) // LANES
    return pl.pallas_call(
        regroup_kernel,
        out_shape=jax.ShapeDtypeStruct((owners * pitch, LANES), jnp.int32),
        in_specs=[
            pl.BlockSpec(memory_space=pltpu.SMEM),
            pl.BlockSpec(memory_space=pltpu.VMEM),
            pl.BlockSpec(memory_space=pltpu.VMEM),
        ],
        out_specs=pl.BlockSpec(memory_space=pltpu.VMEM),
        scratch_shapes=[pltpu.VMEM((rows // 2, channels), jnp.int32)],
        name="regroup",
    )(order, raw, chan_map.reshape(owners, LANES))


def unpack(mixed_ref, words, owners):
    pitch = mixed_ref.shape[0] // owners
    rows = words.shape[1] // owners
    kept = pitch - rows
    for owner in range(owners):
        start = owner * pitch
        words[0, owner * rows : (owner + 1) * rows] = mixed_ref[start + kept : start + pitch, :]
        words[1, owner * rows : (owner + 1) * rows] = mixed_ref[start : start + rows, :]
    lane = lax.broadcasted_iota(jnp.int32, (owners, LANES), 1)
    for row in range(kept, rows):
        whole = jnp.zeros((owners, LANES), jnp.int32)
        for step in range(STEPS):
            target = (row - kept) * STEPS + step
            part = mixed_ref[pl.ds(target, owners, stride=pitch), :]
            part = pltpu.roll(part, (step + 1) * SB, 1)
            whole = jnp.where(lane // SB == step, part, whole)
        words[1, pl.ds(row, owners, stride=rows), :] = whole


def split(value):
    high = value.astype(jnp.bfloat16)
    return high, (value - high.astype(jnp.float32)).astype(jnp.bfloat16)


def correlate_kernel(taps_ref, mixed_ref, out_ref, fetched, xh, xl, white, pair, turned, left, stage, sems):
    half = fetched.shape[1]
    owners = half // HALF_ROWS
    samples = 2 * half
    unpack(mixed_ref, fetched, owners)

    def dot(a, b):
        return jnp.dot(a, b, preferred_element_type=jnp.float32)

    taps = jnp.broadcast_to(taps_ref[0:1, :], (LANES, 2 * LANES))
    band_h, band_l = split(pltpu.roll(taps, 0, 1, stride=1, stride_axis=0))
    band = jnp.concatenate([band_h, band_l, band_h], axis=1)
    edge = jnp.zeros((FIR_HALF, 2 * LANES), jnp.bfloat16)
    for ref in (xh, xl):
        ref[:FIR_HALF] = edge
        ref[FIR_HALF + samples :] = edge
    words = jnp.concatenate([fetched[0], fetched[1]], axis=1).reshape(owners, HALF_ROWS, 2 * LANES)
    values = jnp.concatenate([decode((words << 16) >> 16), decode(words >> 16)], axis=1)
    high, low = split(values.reshape(samples, 2 * LANES))
    xh[FIR_HALF : FIR_HALF + samples] = high
    xl[FIR_HALF : FIR_HALF + samples] = low
    power = jnp.zeros((1, 2 * LANES), jnp.float32)
    for start in range(0, samples, LANES):
        rows = slice(start, start + 2 * LANES)
        piece = dot(band, jnp.concatenate([xl[rows], xh[rows], xh[rows]], axis=0))
        white[start : start + LANES] = piece
        power = power + jnp.sum(piece * piece, axis=0, keepdims=True)
    scale = 1.0 / jnp.sqrt(power * (1.0 / samples) + 1e-06)

    for top in range(0, HALF, SUB):
        gap = jnp.zeros((SUB, 2 * LANES), jnp.bfloat16)
        pair[top : top + SUB] = gap
        pair[samples + HALF - SUB + top : samples + HALF + top] = gap
    pair[samples + 2 * HALF - SUB :] = jnp.zeros((SUB, 2 * LANES), jnp.bfloat16)
    own = (white[:, :LANES] * scale[:, :LANES]).astype(jnp.bfloat16)
    pair[HALF : HALF + samples, :LANES] = own
    pair[HALF - SUB : HALF - SUB + samples, LANES:] = own
    turned[:, :samples] = (white[:, LANES:] * scale[:, LANES:]).astype(jnp.bfloat16).T
    turned[:, samples:] = jnp.zeros((LANES, LANES), jnp.bfloat16)

    gain = 1.0 / math.sqrt(samples)

    def build(step, late, shift):
        source = turned[pl.ds(step * SB, SB), :]
        amount = shift if late else samples + LANES - SUB + shift
        moved = pltpu.roll(source, amount, 1) if amount else source
        left[late, shift * SB : (shift + 1) * SB] = moved[:, :samples]

    def copy(step, index):
        start, stop = SENDS[index]
        rows = pl.ds((step * LAGS + start) * SB, (stop - start) * SB)
        return pltpu.make_async_copy(stage.at[rows, :], out_ref.at[rows, :], sems.at[step, index])

    blocks = HALF // (2 * SUB)
    deep = SUB // PARTS

    for step in range(STEPS):
        for late in range(2):
            for index in range(blocks):
                block = late * HALF + index * 2 * SUB
                first = block if late else block + SUB
                for part in range(PARTS):
                    if step == late == index == 0:
                        for shift in range(part * deep, (part + 1) * deep):
                            build(0, 0, shift)
                    rows = slice(part * deep * SB, (part + 1) * deep * SB)
                    both = dot(left[late, rows], pair[first : first + samples]) * gain
                    low = block + part * deep
                    top = (step * LAGS + low) * SB
                    stage[top : top + deep * SB] = both[:, :LANES]
                    stage[top + SUB * SB : top + (SUB + deep) * SB] = both[:, LANES:]
                if step == late == index == 0:
                    last = dot(turned[: STEPS * SB, :samples], pair[2 * HALF : 2 * HALF + samples, :LANES]) * gain
                    for each in range(STEPS):
                        top = (each * LAGS + LAGS - 1) * SB
                        stage[top : top + SB] = last[each * SB : (each + 1) * SB]
                for shift in range(index * SUB // blocks, (index + 1) * SUB // blocks):
                    build(step + late, 1 - late, shift)
                for piece, (_, stop) in enumerate(SENDS):
                    if stop in (block + 2 * SUB, block + 2 * SUB + 1):
                        copy(step, piece).start()

    for step in range(STEPS):
        for piece in range(len(SENDS)):
            copy(step, piece).wait()


def correlate(fir_taps, mixed, samples):
    taps = jnp.pad(fir_taps, (0, 2 * LANES - fir_taps.shape[0])).reshape(1, 2 * LANES)
    return pl.pallas_call(
        correlate_kernel,
        out_shape=jax.ShapeDtypeStruct((STEPS * LAGS * SB, LANES), jnp.float32),
        in_specs=[pl.BlockSpec(memory_space=pltpu.VMEM)] * 2,
        out_specs=pl.BlockSpec(memory_space=pl.ANY),
        scratch_shapes=[
            pltpu.VMEM((2, samples // 2, LANES), jnp.int32),
            pltpu.VMEM((samples + 2 * FIR_HALF, 2 * LANES), jnp.bfloat16),
            pltpu.VMEM((samples + 2 * FIR_HALF, 2 * LANES), jnp.bfloat16),
            pltpu.VMEM((samples, 2 * LANES), jnp.float32),
            pltpu.VMEM((samples + 2 * HALF, 2 * LANES), jnp.bfloat16),
            pltpu.VMEM((LANES, samples + LANES), jnp.bfloat16),
            pltpu.VMEM((2, SUB * SB, samples), jnp.bfloat16),
            pltpu.VMEM((STEPS * LAGS * SB, LANES), jnp.float32),
            pltpu.SemaphoreType.DMA((STEPS, len(SENDS))),
        ],
        compiler_params=pltpu.CompilerParams(vmem_limit_bytes=48 * 1024 * 1024),
        name="correlate",
    )(taps, mixed)


def local(raw, fir_taps, chan_map, order):
    parts = regroup(raw, chan_map, order)
    rows, channels = raw.shape
    owners = channels // LANES
    parts = parts.reshape(owners, -1, 1, LANES)
    mixed = lax.all_to_all(parts, AXES, split_axis=0, concat_axis=0, tiled=True)
    result = correlate(fir_taps, mixed.reshape(-1, LANES), owners * rows)
    return jnp.transpose(result.reshape(STEPS, LAGS, SB, LANES), (0, 2, 1, 3))


def solution(mesh):
    in_specs = (P(AXES, None), P(), P(), P())
    out_specs = P(None, None, None, AXES)
    return jax.shard_map(local, mesh=mesh, in_specs=in_specs, out_specs=out_specs, check_vma=False)
```
